32 devices in a mesh: groups: 2 (over x), dp: 4 (over z), tensor: 4 (over y, core).
Axes of the slice: x: 2, y: 2, z: 4, core: 2. Of those that a mesh axis runs over, the one named last changes fastest.
Arguments:
- patches: float32 [16, 256, 6144], P(('groups', 'dp'), None, 'tensor'), parts along dimension 0, may hold values from -60 to 60
- counts: int32 [16], P(('groups', 'dp')), parts along dimension 0, may hold values from 1 to 63, as said below
- ranking: int32 [16, 256], P(('groups', 'dp')), parts along dimension 0, may hold values from 0 to 255, each once within a row
- norm_gain: float32 [6144], P('tensor'), may hold values from 0.1 to 1.9
- expand_weight: bfloat16 [24576, 6144], P(('dp', 'tensor')), may hold values from -0.078125 to 0.078125
- expand_bias: bfloat16 [24576], P(('dp', 'tensor')), may hold values from -4 to 4
- reduce_weight: bfloat16 [24576, 6144], P(('dp', 'tensor')), may hold values from -0.078125 to 0.078125
- reduce_bias: float32 [6144], P('tensor'), may hold values from -4 to 4
Outputs:
- updated: float32 [16, 256, 6144], P(('groups', 'dp'), None, 'tensor'), parts along dimension 0
The draws below stay inside these ranges and needn't reach their ends.
There are 2 independent parts, one for each index of `groups`. The reference program is written for one: setup_inputs(seed, part) draws one part's arguments, and reference() takes and returns one part's arrays. A program takes and returns all parts, laid end to end along the dimension named above; an argument that names none is the same for every part. Nothing has to cross between parts.
Inputs may be any that keep to these rules, and one draw needn't show every extreme that they name: The counts of the 2 images of one index of dp (images b * 2 to (b + 1) * 2 - 1) sum to at most 64; in every draw one such group sums to exactly 64, and some image holds exactly 63.
All inputs are finite; a program needn't handle non-finite values.
Results may differ from the reference program's by a relative error of at most 0.00061.
Values may be sent and summed in bfloat16 or wider, within the bound.
A program may use at most 128 MiB of HBM per device.

```python
import jax
import jax.numpy as jnp
from jax import lax

D = 6144
FF = 24576
PATCH = 256
IMG_DEV = 2
CAP = 64
IMAGES = 8


def draw_patches(key, part):
    key_base, key_rows, key_cols = jax.random.split(key, 3)
    ramp = 1.0 + 2.0 * jnp.arange(D, dtype=jnp.float32) / D
    cols = jnp.exp(jax.random.uniform(key_cols, (1, 1, D), jnp.float32, jnp.log(0.5), jnp.log(1.5))) * ramp
    base = jnp.clip(jax.random.normal(key_base, (IMAGES, PATCH, D), jnp.float32), -4.0, 4.0)
    rows = jnp.exp(jax.random.uniform(key_rows, (IMAGES, PATCH, 1), jnp.float32, jnp.log(0.3), jnp.log(3.0)))
    return base * rows * cols


def draw_counts(key, part):
    key_total, key_full, key_share = jax.random.split(jax.random.fold_in(key, 17), 3)
    blocks = IMAGES // IMG_DEV
    totals = jax.random.randint(key_total, (blocks,), IMG_DEV, CAP + 1)
    full = jax.random.randint(key_full, (), 0, blocks)
    totals = jnp.where(jnp.arange(blocks) == full, CAP, totals)
    shares = jax.random.randint(key_share, (blocks, IMG_DEV), 1, 100)
    extra = totals - IMG_DEV
    pieces = 1 + extra[:, None] * shares // jnp.sum(shares, axis=1, keepdims=True)
    rest = totals - jnp.sum(pieces, axis=1)
    pieces = pieces.at[:, 0].add(rest)
    lopsided = jnp.where(jnp.arange(IMG_DEV) == 0, CAP - IMG_DEV + 1, 1)
    pieces = jnp.where((jnp.arange(blocks) == full)[:, None], lopsided[None, :], pieces)
    return pieces.reshape(IMAGES).astype(jnp.int32)


def levels(key, extent, cuts, least, high):
    gain, own = 1.0, jax.random.fold_in(key, 6)
    for position, blocks in cuts:
        steps = jnp.exp(jax.random.uniform(jax.random.fold_in(own, position), (blocks,), jnp.float32, least / len(cuts), high / len(cuts)))
        gain = gain * jnp.repeat(steps, extent[position] // blocks).reshape([-1 if axis == position else 1 for axis in range(len(extent))])
    return gain


def noise(rng, dims, spread, most, cuts=(), kind=jnp.bfloat16):
    loudness = levels(rng, dims, cuts, -0.22, 0.18) if cuts else 1.0
    drawn = jax.random.normal(rng, dims, jnp.float32) * spread * loudness
    return jnp.minimum(jnp.maximum(drawn, -most), most).astype(kind)


def setup_inputs(seed: int = 0, part: int = 0) -> dict:
    seeds = jax.random.split(jax.random.key(seed), 9)
    part_keys = jax.random.split(jax.random.fold_in(seeds[8], part), 9)
    return {
        "patches": draw_patches(jax.random.fold_in(jax.random.fold_in(seeds[8], part), 71), part),
        "counts": draw_counts(jax.random.fold_in(jax.random.fold_in(seeds[8], part), 71), part),
        "ranking": jax.vmap(lambda own: jax.random.permutation(own, PATCH))(jax.random.split(part_keys[2], IMAGES)).reshape((IMAGES, PATCH)).astype(jnp.int32),
        "norm_gain": jnp.clip(1.0 + 0.18 * jax.random.normal(seeds[3], (D,), jnp.float32), 0.1, 1.9),
        "expand_weight": noise(seeds[4], (FF, D), D ** -0.5, 0.078125, ((0, 16),)),
        "expand_bias": noise(seeds[5], (FF,), 0.7, 4.0, ((0, 16),)),
        "reduce_weight": noise(seeds[6], (FF, D), (FF // 4) ** -0.5, 0.078125, ((0, 16),)),
        "reduce_bias": noise(seeds[7], (D,), 0.7, 4.0, ((0, 4),), jnp.float32),
    }


def reference(patches, counts, ranking, norm_gain, expand_weight, expand_bias, reduce_weight, reduce_bias):
    chosen = ranking[:, :CAP].astype(jnp.int32)
    live = jnp.arange(CAP, dtype=jnp.int32)[None, :] < counts[:, None]
    rows = jnp.take_along_axis(patches, chosen[:, :, None], axis=1)
    flat = rows.reshape(IMAGES * CAP, D)
    first = lax.optimization_barrier(jnp.sum(flat, axis=1, keepdims=True))
    second = lax.optimization_barrier(jnp.sum(flat * flat, axis=1, keepdims=True))
    mean = first / D
    var = second / D - mean * mean
    normed = ((flat - mean) * lax.rsqrt(var + 1e-06) * norm_gain).astype(jnp.bfloat16)
    pre = lax.dot_general(normed, expand_weight, (((1,), (1,)), ((), ())), preferred_element_type=jnp.float32)
    pre = pre + expand_bias.astype(jnp.float32)
    hidden = jax.nn.gelu(pre, approximate=True).astype(jnp.bfloat16)
    branch = jnp.dot(hidden, reduce_weight, preferred_element_type=jnp.float32)
    update = flat + (branch + reduce_bias)
    update = jnp.where(live.reshape(IMAGES * CAP)[:, None], update, flat).reshape(IMAGES, CAP, D)
    image_index = jnp.arange(IMAGES, dtype=jnp.int32)[:, None]
    return patches.at[image_index, chosen].set(update)
```

```python
import functools

import jax
import jax.numpy as jnp
from jax import lax
from jax.experimental import pallas as pl
from jax.experimental.pallas import tpu as pltpu
from jax.sharding import PartitionSpec as P

CAP = 64
MESH = pl.DeviceIdType.MESH


def gather_kernel(counts, ranking, flat, rows, sem):
    images, patch_len = ranking.shape

    def issue(j, carry):
        start, source = 0, 0
        for i in range(images):
            offset = j - start
            inside = (offset >= 0) & (offset < counts[i])
            place = ranking[i, jnp.clip(offset, 0, patch_len - 1)]
            source = jnp.where(inside, i * patch_len + place, source)
            start = start + counts[i]
        pltpu.make_async_copy(flat.at[pl.ds(source, 1)], rows.at[pl.ds(j, 1)], sem).start()
        return carry

    lax.fori_loop(0, CAP, issue, 0)
    pltpu.make_async_copy(rows, rows, sem).wait()


def update_kernel(counts, ranking, flat, update, out, buf, in_sem, out_sem):
    images, patch_len = ranking.shape

    def load(i):
        part = pl.ds(i * patch_len, patch_len)
        return pltpu.make_async_copy(flat.at[part], buf.at[part], in_sem.at[i])

    def save(i):
        part = pl.ds(i * patch_len, patch_len)
        return pltpu.make_async_copy(buf.at[part], out.at[part], out_sem.at[i])

    for i in range(images):
        load(i).start()
    start = 0
    for i in range(images):
        load(i).wait()

        def put(j, carry):
            buf[pl.ds(i * patch_len + ranking[i, j], 1), :] = update[pl.ds(carry + j, 1), :]
            return carry

        lax.fori_loop(0, counts[i], put, start)
        start = start + counts[i]
        save(i).start()
    for i in range(images):
        save(i).wait()


def block_kernel(
    Z, T, C, C2, rows, gain, ebias, rbias, e_hbm, r_hbm, out,
    xg, wv, rv, pre, hid, st, cs, cr, own, ys, yr, zs, zr,
    wsem, rsem, st_s, st_r, za_s, za_r, ya_s, ya_r, ca_s, ca_r,
    cr_s, cr_r, yr_s, yr_r, zr_s, zr_r,
):
    Y = T // 2
    R, dl = rows.shape
    hl, D = e_hbm.shape
    M, dlc, w2 = Z * R, dl // C, dl // C2
    nt = 256 if hl % 256 == 0 else hl
    z = lax.axis_index("dp")
    t = lax.axis_index("tensor")
    y, c = t // 2, t % 2
    z_next = lax.rem(z + 1, Z)
    t_next = lax.rem(y + 1, Y) * 2 + c
    t_part = y * 2 + 1 - c

    barrier = pltpu.get_barrier_semaphore()
    for k in range(1, Z):
        pl.semaphore_signal(barrier, inc=1, device_id={"dp": lax.rem(z + k, Z)}, device_id_type=MESH)
    for k in range(1, T):
        pl.semaphore_signal(barrier, inc=1, device_id={"tensor": lax.rem(t + k, T)}, device_id_type=MESH)

    def copy(src, dst, ss, rs, axis, index):
        return pltpu.make_async_remote_copy(
            src_ref=src, dst_ref=dst, send_sem=ss, recv_sem=rs,
            device_id={axis: index}, device_id_type=MESH,
        )

    def t_of(u, core):
        return lax.rem(y - u + Y, Y) * 2 + core

    def t_red(u, core):
        return lax.rem(y - 1 - u + 2 * Y, Y) * 2 + core

    order = []
    for u in range(Y):
        for core in (c, 1 - c):
            for p in range(C):
                order.append((t_of(u, core), p))

    def expand_load(i):
        block, p = order[i]
        lanes = pl.ds(pl.multiple_of(block * dl + p * dlc, 128), dlc)
        return pltpu.make_async_copy(e_hbm.at[:, lanes], wv.at[i], wsem.at[i])

    def reduce_load(i):
        block = t_red(i // 2, c if i % 2 == 0 else 1 - c)
        lanes = pl.ds(pl.multiple_of(block * dl, 128), dl)
        return pltpu.make_async_copy(r_hbm.at[:, lanes], rv.at[i], rsem.at[i])

    for i in range(T * C):
        expand_load(i).start()
    for i in range(T):
        reduce_load(i).start()

    x = rows[...]
    s1 = jnp.sum(x, axis=1, keepdims=True)
    s2 = jnp.sum(x * x, axis=1, keepdims=True)
    lane = lax.broadcasted_iota(jnp.int32, (R, 128), 1)
    st[t] = jnp.where(lane == 0, s1, s2)
    pl.semaphore_wait(barrier, Z + T - 2)

    def stat_copy(k):
        return copy(st.at[t], st.at[t], st_s.at[k - 1], st_r.at[k - 1], "tensor", lax.rem(t + k, T))

    for k in range(1, T):
        stat_copy(k).start()
    for k in range(1, T):
        stat_copy(k).wait_recv()
    total = st[0]
    for k in range(1, T):
        total = total + st[k]
    mean = total[:, 0:1] / D
    var = total[:, 1:2] / D - mean * mean
    scale = lax.rsqrt(var + 1e-06)
    mine = pl.ds(pl.multiple_of(z * R, R), R)
    for p in range(C):
        cols = slice(p * dlc, (p + 1) * dlc)
        xg[t, p, mine, :] = ((rows[:, cols] - mean) * scale * gain[:, cols]).astype(jnp.bfloat16)

    def block(tt, j, p):
        return xg.at[tt, p, pl.ds(pl.multiple_of(lax.rem(z - j + Z, Z) * R, R), R), :]

    def z_copy(s, p):
        b = block(t, s - 1, p)
        return copy(b, b, za_s.at[s - 1, p], za_r.at[s - 1, p], "dp", z_next)

    def y_copy(u, j, p):
        b = block(t_of(u - 1, c), j, p)
        return copy(b, b, ya_s.at[u - 1, j, p], ya_r.at[u - 1, j, p], "tensor", t_next)

    def c_copy(u, j, p):
        b = block(t_of(u, c), j, p)
        return copy(b, b, ca_s.at[u, j, p], ca_r.at[u, j, p], "tensor", t_part)

    def expand(i):
        tt, p = order[i]
        expand_load(i).wait()

        def tile(n):
            cols = slice(None) if nt == hl else pl.ds(pl.multiple_of(n * nt, nt), nt)
            acc = lax.dot_general(
                xg[tt, p], wv[i, cols, :], (((1,), (1,)), ((), ())),
                preferred_element_type=jnp.float32,
            )
            if i > 0:
                acc = acc + pre[:, cols]
            if i < T * C - 1:
                pre[:, cols] = acc
            else:
                v = acc + ebias[:, cols].astype(jnp.float32)
                hid[:, cols] = jax.nn.gelu(v, approximate=True).astype(jnp.bfloat16)

        if nt == hl:
            tile(0)
        else:
            lax.fori_loop(0, hl // nt, lambda n, a: (tile(n), a)[1], 0)

    def expand_partner(u, p):
        for j in range(Z):
            c_copy(u, j, p).wait_recv()
        expand((2 * u + 1) * C + p)

    def y_arrived(u, j, p):
        y_copy(u, j, p).wait_recv()
        if u < Y - 1:
            y_copy(u + 1, j, p).start()
        c_copy(u, j, p).start()

    for p in range(C):
        z_copy(1, p).start()
        y_copy(1, 0, p).start()
        c_copy(0, 0, p).start()
    for s in range(1, Z):
        for p in range(C):
            z_copy(s, p).wait_recv()
            if s < Z - 1:
                z_copy(s + 1, p).start()
            y_copy(1, s, p).start()
            c_copy(0, s, p).start()
            if s == Z - 1:
                expand(p)
        for p in range(C):
            y_arrived(1, s - 1, p)
    for p in range(C):
        expand_partner(0, p)
    for u in range(1, Y):
        for j in range(Z - 1 if u == 1 else 0, Z):
            for p in range(C):
                y_arrived(u, j, p)
                if j == Z - 1:
                    expand(2 * u * C + p)
        for p in range(C):
            expand_partner(u, p)

    def cr_copy(u, p):
        return copy(cs.at[u, p], cr.at[u, p], cr_s.at[u, p], cr_r.at[u, p], "tensor", t_part)

    def yr_copy(u, p):
        return copy(ys.at[u - 1, p], yr.at[u - 1, p], yr_s.at[u - 1, p], yr_r.at[u - 1, p], "tensor", t_next)

    def zr_copy(k, p):
        there = lax.rem(z + k, Z)
        part = pl.ds(pl.multiple_of(there * R, R), R)
        return copy(zs.at[p, part, :], zr.at[k - 1, p], zr_s.at[k - 1, p], zr_r.at[k - 1, p], "dp", there)

    def columns(p):
        return slice(None) if C2 == 1 else pl.ds(pl.multiple_of(p * w2, w2), w2)

    def product(i, p):
        return jnp.dot(hid[...], rv[i, :, columns(p)], preferred_element_type=jnp.float32)

    def produce(u, p):
        cs[u, p] = product(2 * u + 1, p).astype(jnp.bfloat16)
        cr_copy(u, p).start()
        own[u, p] = product(2 * u, p)

    def combine(u, p):
        cr_copy(u, p).wait_recv()
        v = own[u, p] + cr[u, p].astype(jnp.float32)
        if u == 0:
            ys[0, p] = v.astype(jnp.bfloat16)
            yr_copy(1, p).start()
        else:
            own[u, p] = v

    def loop(low, high, body):
        lax.fori_loop(low, high, lambda p, a: (body(p), a)[1], 0)

    for u in range(Y):
        reduce_load(2 * u).wait()
        reduce_load(2 * u + 1).wait()
        produce(u, 0)
        if u > 0:
            combine(u - 1, C2 - 1)

        def step(p):
            produce(u, p)
            combine(u, p - 1)

        if C2 > 1:
            loop(1, C2, step)
    combine(Y - 1, C2 - 1)

    for u in range(1, Y):

        def pass_on(p):
            yr_copy(u, p).wait_recv()
            v = own[u, p] + yr[u - 1, p].astype(jnp.float32)
            if u < Y - 1:
                ys[u, p] = v.astype(jnp.bfloat16)
                yr_copy(u + 1, p).start()
            else:
                own[u, p] = v
                zs[p] = v.astype(jnp.bfloat16)
                for k in range(1, Z):
                    zr_copy(k, p).start()

        loop(0, C2, pass_on)

    def finish(p):
        acc = own[Y - 1, p, mine, :]
        for k in range(1, Z):
            zr_copy(k, p).wait_recv()
            acc = acc + zr[k - 1, p].astype(jnp.float32)
        cols = columns(p)
        out[:, cols] = rows[:, cols] + (acc + rbias[:, cols])

    loop(0, C2, finish)

    for k in range(1, T):
        stat_copy(k).wait_send()
    for p in range(C):
        for s in range(1, Z):
            z_copy(s, p).wait_send()
        for j in range(Z):
            for u in range(1, Y):
                y_copy(u, j, p).wait_send()
            for u in range(Y):
                c_copy(u, j, p).wait_send()

    def drain(p):
        for u in range(Y):
            cr_copy(u, p).wait_send()
        for u in range(1, Y):
            yr_copy(u, p).wait_send()
        for k in range(1, Z):
            zr_copy(k, p).wait_send()

    loop(0, C2, drain)


def body(
    Z, T, patches, counts, ranking, norm_gain, expand_weight, expand_bias, reduce_weight, reduce_bias
):
    images, patch_len, dl = patches.shape
    hl, D = expand_weight.shape
    flat = patches.reshape(images * patch_len, dl)
    R, M, Y = CAP, Z * CAP, T // 2
    C = 3 if dl % 768 == 0 else 1
    w2 = 256 if dl % 256 == 0 else dl
    C2 = dl // w2
    dlc = dl // C
    vmem = pl.BlockSpec(memory_space=pltpu.VMEM)
    hbm = pl.BlockSpec(memory_space=pl.ANY)
    bf16, f32 = jnp.bfloat16, jnp.float32
    rows = pl.pallas_call(
        gather_kernel,
        out_shape=jax.ShapeDtypeStruct((R, dl), f32),
        grid_spec=pltpu.PrefetchScalarGridSpec(
            num_scalar_prefetch=2, grid=(), in_specs=[hbm], out_specs=vmem,
            scratch_shapes=[pltpu.SemaphoreType.DMA],
        ),
        name="gather_rows",
    )(counts, ranking, flat)
    dma = pltpu.SemaphoreType.DMA
    update = pl.pallas_call(
        functools.partial(block_kernel, Z, T, C, C2),
        out_shape=jax.ShapeDtypeStruct((R, dl), f32),
        in_specs=[vmem] * 4 + [hbm] * 2,
        out_specs=vmem,
        scratch_shapes=[
            pltpu.VMEM((T, C, M, dlc), bf16),
            pltpu.VMEM((T * C, hl, dlc), bf16),
            pltpu.VMEM((T, hl, dl), bf16),
            pltpu.VMEM((M, hl), f32),
            pltpu.VMEM((M, hl), bf16),
            pltpu.VMEM((T, R, 128), f32),
            pltpu.VMEM((Y, C2, M, w2), bf16),
            pltpu.VMEM((Y, C2, M, w2), bf16),
            pltpu.VMEM((Y, C2, M, w2), f32),
            pltpu.VMEM((Y - 1, C2, M, w2), bf16),
            pltpu.VMEM((Y - 1, C2, M, w2), bf16),
            pltpu.VMEM((C2, M, w2), bf16),
            pltpu.VMEM((Z - 1, C2, R, w2), bf16),
            dma((T * C,)), dma((T,)),
            dma((T - 1,)), dma((T - 1,)),
            dma((Z - 1, C)), dma((Z - 1, C)),
            dma((Y - 1, Z, C)), dma((Y - 1, Z, C)),
            dma((Y, Z, C)), dma((Y, Z, C)),
            dma((Y, C2)), dma((Y, C2)),
            dma((Y - 1, C2)), dma((Y - 1, C2)),
            dma((Z - 1, C2)), dma((Z - 1, C2)),
        ],
        compiler_params=pltpu.CompilerParams(
            collective_id=0, has_side_effects=True, vmem_limit_bytes=67000000
        ),
        name="feed_forward",
    )(
        rows, norm_gain.reshape(1, dl), expand_bias.reshape(1, hl), reduce_bias.reshape(1, dl),
        expand_weight, reduce_weight,
    )
    result = pl.pallas_call(
        update_kernel,
        out_shape=jax.ShapeDtypeStruct((images * patch_len, dl), f32),
        grid_spec=pltpu.PrefetchScalarGridSpec(
            num_scalar_prefetch=2, grid=(), in_specs=[hbm, vmem], out_specs=hbm,
            scratch_shapes=[
                pltpu.VMEM((images * patch_len, dl), f32),
                dma((images,)), dma((images,)),
            ],
        ),
        name="update_rows",
    )(counts, ranking, flat, update)
    return result.reshape(images, patch_len, dl)


def solution(mesh):
    placed = (
        P(("groups", "dp"), None, "tensor"),
        P(("groups", "dp")),
        P(("groups", "dp"), None),
        P("tensor"),
        P(("dp", "tensor"), None),
        P(("dp", "tensor")),
        P(("dp", "tensor"), None),
        P("tensor"),
    )
    return jax.shard_map(
        functools.partial(body, mesh.shape["dp"], mesh.shape["tensor"]),
        mesh=mesh,
        in_specs=placed,
        out_specs=P(("groups", "dp"), None, "tensor"),
        check_vma=False,
    )
```

```python
import functools

import jax
import jax.numpy as jnp
from jax import lax
from jax.experimental import pallas as pl
from jax.experimental.pallas import tpu as pltpu
from jax.sharding import PartitionSpec as P

CAP = 64
MESH = pl.DeviceIdType.MESH


def block_kernel(
    Z, T, C, C2, counts, ranking, ranking_v, gain, ebias, rbias, flat, e_hbm, r_hbm, out,
    pt, rows, pick,    xg, wv, rv, pre, hid, bias, last, st, cs, cr, own, ys, yr, zs, zr,
    psem, osem, wsem, rsem, st_s, st_r, za_s, za_r, ya_s, ya_r, ca_s, ca_r,
    cr_s, cr_r, yr_s, yr_r, zr_s, zr_r,
):
    Y = T // 2
    R, dl = rows.shape
    images, patch_len = ranking.shape
    N = images * patch_len
    hl, D = e_hbm.shape
    M, dlc, w2 = Z * R, dl // C, dl // C2
    nt = 256 if hl % 256 == 0 else hl
    z = lax.axis_index("dp")
    t = lax.axis_index("tensor")
    y, c = t // 2, t % 2
    z_next = lax.rem(z + 1, Z)
    t_next = lax.rem(y + 1, Y) * 2 + c
    t_part = y * 2 + 1 - c

    barrier = pltpu.get_barrier_semaphore()
    for k in range(1, Z):
        pl.semaphore_signal(barrier, inc=1, device_id={"dp": lax.rem(z + k, Z)}, device_id_type=MESH)
    for k in range(1, T):
        pl.semaphore_signal(barrier, inc=1, device_id={"tensor": lax.rem(t + k, T)}, device_id_type=MESH)

    def copy(src, dst, ss, rs, axis, index):
        return pltpu.make_async_remote_copy(
            src_ref=src, dst_ref=dst, send_sem=ss, recv_sem=rs,
            device_id={axis: index}, device_id_type=MESH,
        )

    def t_of(u, core):
        return lax.rem(y - u + Y, Y) * 2 + core

    def t_red(u, core):
        return lax.rem(y - 1 - u + 2 * Y, Y) * 2 + core

    order = []
    for u in range(Y):
        for core in (c, 1 - c):
            for p in range(C):
                order.append((t_of(u, core), p))

    def expand_load(i):
        block, p = order[i]
        lanes = pl.ds(pl.multiple_of(block * dl + p * dlc, 128), dlc)
        return pltpu.make_async_copy(e_hbm.at[:, lanes], wv.at[i], wsem.at[i])

    def reduce_load(i):
        block = t_red(i // 2, c if i % 2 == 0 else 1 - c)
        lanes = pl.ds(pl.multiple_of(block * dl, 128), dl)
        return pltpu.make_async_copy(r_hbm.at[:, lanes], rv.at[i], rsem.at[i])

    patch_load = pltpu.make_async_copy(flat, pt, psem)
    patch_load.start()

    lane_w = images * R
    which = lax.broadcasted_iota(jnp.int32, (1, lane_w), 1)
    rank, owner = jnp.full((1, lane_w), -1, jnp.int32), jnp.full((1, lane_w), -1, jnp.int32)
    start = 0
    for i in range(images):
        k = which - i * R
        live = (k >= 0) & (k < counts[i])
        owner = jnp.where(live, start + k, owner)
        start = start + counts[i]
        known = jnp.concatenate([ranking_v[i : i + 1, :R]] * images, axis=1)
        rank = jnp.where(live, i * patch_len + known, rank)
    chosen = jnp.where(lax.broadcasted_iota(jnp.int32, (N, lane_w), 0) == rank, 1.0, 0.0)
    slot = jnp.where(lax.broadcasted_iota(jnp.int32, (R, lane_w), 0) == owner, 1.0, 0.0)
    pick[...] = lax.dot_general(
        chosen.astype(jnp.bfloat16), slot.astype(jnp.bfloat16), (((1,), (1,)), ((), ())),
        preferred_element_type=jnp.float32,
    ).astype(jnp.bfloat16)

    def take(j, carry):
        start, source = 0, 0
        for i in range(images):
            offset = j - start
            inside = (offset >= 0) & (offset < counts[i])
            here = i * patch_len + ranking[i, jnp.clip(offset, 0, patch_len - 1)]
            source = jnp.where(inside, here, source)
            start = start + counts[i]
        rows[pl.ds(j, 1), :] = pt[pl.ds(source, 1), :]
        return carry

    patch_load.wait()
    for i in range(T * C):
        expand_load(i).start()
    for i in range(T):
        reduce_load(i).start()
    lax.fori_loop(0, R, take, 0, unroll=8)

    bias[...] = ebias[...].astype(jnp.float32)[None, :]
    x = rows[...]
    s1 = jnp.sum(x, axis=1, keepdims=True)
    s2 = jnp.sum(x * x, axis=1, keepdims=True)
    lane = lax.broadcasted_iota(jnp.int32, (R, 128), 1)
    st[t] = jnp.where(lane == 0, s1, s2)
    pl.semaphore_wait(barrier, Z + T - 2)

    def stat_copy(k):
        return copy(st.at[t], st.at[t], st_s.at[k - 1], st_r.at[k - 1], "tensor", lax.rem(t + k, T))

    for k in range(1, T):
        stat_copy(k).start()
    for k in range(1, T):
        stat_copy(k).wait_recv()
    total = st[0]
    for k in range(1, T):
        total = total + st[k]
    gain_row = gain[...][None, :]
    mean = total[:, 0:1] / D
    var = total[:, 1:2] / D - mean * mean
    scale = lax.rsqrt(var + 1e-06)
    mine = pl.ds(pl.multiple_of(z * R, R), R)
    for p in range(C):
        cols = slice(p * dlc, (p + 1) * dlc)
        xg[t, p, mine, :] = ((rows[:, cols] - mean) * scale * gain_row[:, cols]).astype(jnp.bfloat16)

    def block(tt, j, p):
        return xg.at[tt, p, pl.ds(pl.multiple_of(lax.rem(z - j + Z, Z) * R, R), R), :]

    def z_copy(s, p):
        b = block(t, s - 1, p)
        return copy(b, b, za_s.at[s - 1, p], za_r.at[s - 1, p], "dp", z_next)

    def y_copy(u, j, p):
        b = block(t_of(u - 1, c), j, p)
        return copy(b, b, ya_s.at[u - 1, j, p], ya_r.at[u - 1, j, p], "tensor", t_next)

    def c_copy(u, j, p):
        b = block(t_of(u, c), j, p)
        return copy(b, b, ca_s.at[u, j, p], ca_r.at[u, j, p], "tensor", t_part)

    def expand(i):
        tt, p = order[i]
        expand_load(i).wait()

        acc = lax.dot_general(
            wv[i], xg[tt, p], (((1,), (1,)), ((), ())), preferred_element_type=jnp.float32
        )
        pre[...] = acc if i == 0 else pre[...] + acc

    def expand_partner(u, p):
        for j in range(Z):
            c_copy(u, j, p).wait_recv()
        expand((2 * u + 1) * C + p)

    def y_arrived(u, j, p):
        y_copy(u, j, p).wait_recv()
        if u < Y - 1:
            y_copy(u + 1, j, p).start()
        c_copy(u, j, p).start()

    for p in range(C):
        z_copy(1, p).start()
        y_copy(1, 0, p).start()
        c_copy(0, 0, p).start()
    for s in range(1, Z):
        for p in range(C):
            z_copy(s, p).wait_recv()
            if s < Z - 1:
                z_copy(s + 1, p).start()
            y_copy(1, s, p).start()
            c_copy(0, s, p).start()
            if s == Z - 1:
                expand(p)
        for p in range(C):
            y_arrived(1, s - 1, p)
    for p in range(C):
        expand_partner(0, p)
    for u in range(1, Y):
        for j in range(Z - 1 if u == 1 else 0, Z):
            for p in range(C):
                y_arrived(u, j, p)
                if j == Z - 1:
                    expand(2 * u * C + p)
        for p in range(C):
            expand_partner(u, p)

    def activate(n):
        units = slice(None) if nt == hl else pl.ds(pl.multiple_of(n * nt, nt), nt)
        v = pre[units, :].T + bias[:, units]
        hid[:, units] = jax.nn.gelu(v, approximate=True).astype(jnp.bfloat16)

    if nt == hl:
        activate(0)
    else:
        lax.fori_loop(0, hl // nt, lambda n, a: (activate(n), a)[1], 0)

    def cr_copy(u, p):
        return copy(cs.at[u, p], cr.at[u, p], cr_s.at[u, p], cr_r.at[u, p], "tensor", t_part)

    def yr_copy(u, p):
        return copy(ys.at[u - 1, p], yr.at[u - 1, p], yr_s.at[u - 1, p], yr_r.at[u - 1, p], "tensor", t_next)

    def zr_copy(k, p):
        there = lax.rem(z + k, Z)
        part = pl.ds(pl.multiple_of(there * R, R), R)
        return copy(zs.at[p, part, :], zr.at[k - 1, p], zr_s.at[k - 1, p], zr_r.at[k - 1, p], "dp", there)

    def columns(p):
        return slice(None) if C2 == 1 else pl.ds(pl.multiple_of(p * w2, w2), w2)

    def product(i, p):
        return jnp.dot(hid[...], rv[i, :, columns(p)], preferred_element_type=jnp.float32)

    def produce(u, p):
        cs[u, p] = product(2 * u + 1, p).astype(jnp.bfloat16)
        cr_copy(u, p).start()
        own[u, p] = product(2 * u, p)

    def combine(u, p):
        cr_copy(u, p).wait_recv()
        v = own[u, p] + cr[u, p].astype(jnp.float32)
        if u == 0:
            ys[0, p] = v.astype(jnp.bfloat16)
            yr_copy(1, p).start()
        else:
            own[u, p] = v

    def loop(low, high, body):
        lax.fori_loop(low, high, lambda p, a: (body(p), a)[1], 0)

    for u in range(Y):
        reduce_load(2 * u).wait()
        reduce_load(2 * u + 1).wait()
        produce(u, 0)
        if u > 0:
            combine(u - 1, C2 - 1)

        def step(p):
            produce(u, p)
            combine(u, p - 1)

        if C2 > 1:
            loop(1, C2, step)
    combine(Y - 1, C2 - 1)

    for u in range(1, Y):

        def pass_on(p):
            yr_copy(u, p).wait_recv()
            v = own[u, p] + yr[u - 1, p].astype(jnp.float32)
            if u < Y - 1:
                ys[u, p] = v.astype(jnp.bfloat16)
                yr_copy(u + 1, p).start()
            else:
                own[u, p] = v
                zs[p] = v.astype(jnp.bfloat16)
                for k in range(1, Z):
                    zr_copy(k, p).start()

        loop(0, C2, pass_on)

    last[...] = rbias[...][None, :]

    def finish(p):
        acc = own[Y - 1, p, mine, :]
        for k in range(1, Z):
            zr_copy(k, p).wait_recv()
            acc = acc + zr[k - 1, p].astype(jnp.float32)
        cols = columns(p)
        add = acc + last[:, cols]
        top = add.astype(jnp.bfloat16)
        rest = add - top.astype(jnp.float32)
        middle = rest.astype(jnp.bfloat16)
        low = (rest - middle.astype(jnp.float32)).astype(jnp.bfloat16)
        spread = jnp.dot(pick[...], low, preferred_element_type=jnp.float32)
        spread = spread + jnp.dot(pick[...], middle, preferred_element_type=jnp.float32)
        spread = spread + jnp.dot(pick[...], top, preferred_element_type=jnp.float32)
        pt[:, cols] = pt[:, cols] + spread
        save(p).start()

    def save(p):
        cols = columns(p)
        return pltpu.make_async_copy(pt.at[:, cols], out.at[:, cols], osem.at[p])

    loop(0, C2, finish)

    for k in range(1, T):
        stat_copy(k).wait_send()
    for p in range(C):
        for s in range(1, Z):
            z_copy(s, p).wait_send()
        for j in range(Z):
            for u in range(1, Y):
                y_copy(u, j, p).wait_send()
            for u in range(Y):
                c_copy(u, j, p).wait_send()

    def drain(p):
        save(p).wait()
        for u in range(Y):
            cr_copy(u, p).wait_send()
        for u in range(1, Y):
            yr_copy(u, p).wait_send()
        for k in range(1, Z):
            zr_copy(k, p).wait_send()

    loop(0, C2, drain)


def body(
    Z, T, patches, counts, ranking, norm_gain, expand_weight, expand_bias, reduce_weight, reduce_bias
):
    images, patch_len, dl = patches.shape
    hl, D = expand_weight.shape
    flat = patches.reshape(images * patch_len, dl)
    R, M, Y = CAP, Z * CAP, T // 2
    C = 3 if dl % 768 == 0 else 1
    w2 = 384 if dl % 384 == 0 else dl
    C2 = dl // w2
    dlc = dl // C
    vmem = pl.BlockSpec(memory_space=pltpu.VMEM)
    hbm = pl.BlockSpec(memory_space=pl.ANY)
    bf16, f32 = jnp.bfloat16, jnp.float32
    dma = pltpu.SemaphoreType.DMA
    N = images * patch_len
    smem = pl.BlockSpec(memory_space=pltpu.SMEM)
    result = pl.pallas_call(
        functools.partial(block_kernel, Z, T, C, C2),
        out_shape=jax.ShapeDtypeStruct((N, dl), f32),
        in_specs=[smem] * 2 + [vmem] * 4 + [hbm] * 3,
        out_specs=hbm,
        scratch_shapes=[
            pltpu.VMEM((N, dl), f32),
            pltpu.VMEM((R, dl), f32),
            pltpu.VMEM((N, R), bf16),
            pltpu.VMEM((T, C, M, dlc), bf16),
            pltpu.VMEM((T * C, hl, dlc), bf16),
            pltpu.VMEM((T, hl, dl), bf16),
            pltpu.VMEM((hl, M), f32),
            pltpu.VMEM((M, hl), bf16),
            pltpu.VMEM((1, hl), f32),
            pltpu.VMEM((1, dl), f32),
            pltpu.VMEM((T, R, 128), f32),
            pltpu.VMEM((Y, C2, M, w2), bf16),
            pltpu.VMEM((Y, C2, M, w2), bf16),
            pltpu.VMEM((Y, C2, M, w2), f32),
            pltpu.VMEM((Y - 1, C2, M, w2), bf16),
            pltpu.VMEM((Y - 1, C2, M, w2), bf16),
            pltpu.VMEM((C2, M, w2), bf16),
            pltpu.VMEM((Z - 1, C2, R, w2), bf16),
            dma, dma((C2,)), dma((T * C,)), dma((T,)),
            dma((T - 1,)), dma((T - 1,)),
            dma((Z - 1, C)), dma((Z - 1, C)),
            dma((Y - 1, Z, C)), dma((Y - 1, Z, C)),
            dma((Y, Z, C)), dma((Y, Z, C)),
            dma((Y, C2)), dma((Y, C2)),
            dma((Y - 1, C2)), dma((Y - 1, C2)),
            dma((Z - 1, C2)), dma((Z - 1, C2)),
        ],
        compiler_params=pltpu.CompilerParams(
            collective_id=0, has_side_effects=True, vmem_limit_bytes=67000000
        ),
        name="feed_forward",
    )(
        counts, ranking, ranking, norm_gain, expand_bias, reduce_bias, flat, expand_weight, reduce_weight,
    )
    return result.reshape(images, patch_len, dl)


def solution(mesh):
    placed = (
        P(("groups", "dp"), None, "tensor"),
        P(("groups", "dp")),
        P(("groups", "dp"), None),
        P("tensor"),
        P(("dp", "tensor"), None),
        P(("dp", "tensor")),
        P(("dp", "tensor"), None),
        P("tensor"),
    )
    return jax.shard_map(
        functools.partial(body, mesh.shape["dp"], mesh.shape["tensor"]),
        mesh=mesh,
        in_specs=placed,
        out_specs=P(("groups", "dp"), None, "tensor"),
        check_vma=False,
    )
```

```python
import functools

import jax
import jax.numpy as jnp
from jax import lax
from jax.experimental import pallas as pl
from jax.experimental.pallas import tpu as pltpu
from jax.sharding import PartitionSpec as P

CAP = 64
MESH = pl.DeviceIdType.MESH


def block_kernel(
    Z, T, C, C2, counts, ranking, ranking_v, gain, ebias, rbias, flat, e_hbm, r_hbm, out,
    pt, rows, pick,    xg, wv, rv, pre, hid, bias, last, st, cs, cr, own, ys, yr, zs, zr,
    psem, osem, wsem, rsem, st_s, st_r, za_s, za_r, ya_s, ya_r, ca_s, ca_r,
    cr_s, cr_r, yr_s, yr_r, zr_s, zr_r,
):
    Y = T // 2
    R, dl = rows.shape
    images, patch_len = ranking.shape
    N = images * patch_len
    hl, D = e_hbm.shape
    M, dlc, w2 = Z * R, dl // C, dl // C2
    nt = 256 if hl % 256 == 0 else hl
    z = lax.axis_index("dp")
    t = lax.axis_index("tensor")
    y, c = t // 2, t % 2
    z_next = lax.rem(z + 1, Z)
    t_next = lax.rem(y + 1, Y) * 2 + c
    t_part = y * 2 + 1 - c

    barrier = pltpu.get_barrier_semaphore()
    for k in range(1, Z):
        pl.semaphore_signal(barrier, inc=1, device_id={"dp": lax.rem(z + k, Z)}, device_id_type=MESH)
    for k in range(1, T):
        pl.semaphore_signal(barrier, inc=1, device_id={"tensor": lax.rem(t + k, T)}, device_id_type=MESH)

    def copy(src, dst, ss, rs, axis, index):
        return pltpu.make_async_remote_copy(
            src_ref=src, dst_ref=dst, send_sem=ss, recv_sem=rs,
            device_id={axis: index}, device_id_type=MESH,
        )

    def t_of(u, core):
        return lax.rem(y - u + Y, Y) * 2 + core

    def t_red(u, core):
        return lax.rem(y - 1 - u + 2 * Y, Y) * 2 + core

    order = []
    for u in range(Y):
        for core in (c, 1 - c):
            for p in range(C):
                order.append((t_of(u, core), p))

    def expand_load(i):
        block, p = order[i]
        lanes = pl.ds(pl.multiple_of(block * dl + p * dlc, 128), dlc)
        return pltpu.make_async_copy(e_hbm.at[:, lanes], wv.at[i], wsem.at[i])

    def reduce_load(i):
        block = t_red(i // 2, c if i % 2 == 0 else 1 - c)
        lanes = pl.ds(pl.multiple_of(block * dl, 128), dl)
        return pltpu.make_async_copy(r_hbm.at[:, lanes], rv.at[i], rsem.at[i])

    patch_load = pltpu.make_async_copy(flat, pt, psem)
    patch_load.start()

    lane_w = images * R
    which = lax.broadcasted_iota(jnp.int32, (1, lane_w), 1)
    rank, owner = jnp.full((1, lane_w), -1, jnp.int32), jnp.full((1, lane_w), -1, jnp.int32)
    start = 0
    for i in range(images):
        k = which - i * R
        live = (k >= 0) & (k < counts[i])
        owner = jnp.where(live, start + k, owner)
        start = start + counts[i]
        known = jnp.concatenate([ranking_v[i : i + 1, :R]] * images, axis=1)
        rank = jnp.where(live, i * patch_len + known, rank)
    chosen = jnp.where(lax.broadcasted_iota(jnp.int32, (N, lane_w), 0) == rank, 1.0, 0.0)
    slot = jnp.where(lax.broadcasted_iota(jnp.int32, (R, lane_w), 0) == owner, 1.0, 0.0)
    pick[...] = lax.dot_general(
        chosen.astype(jnp.bfloat16), slot.astype(jnp.bfloat16), (((1,), (1,)), ((), ())),
        preferred_element_type=jnp.float32,
    ).astype(jnp.bfloat16)

    def take(j, carry):
        start, source = 0, 0
        for i in range(images):
            offset = j - start
            inside = (offset >= 0) & (offset < counts[i])
            here = i * patch_len + ranking[i, jnp.clip(offset, 0, patch_len - 1)]
            source = jnp.where(inside, here, source)
            start = start + counts[i]
        rows[pl.ds(j, 1), :] = pt[pl.ds(source, 1), :]
        return carry

    patch_load.wait()
    for i in range(T * C):
        expand_load(i).start()
    for i in range(T):
        reduce_load(i).start()
    lax.fori_loop(0, R, take, 0, unroll=8)

    bias[...] = ebias[...].astype(jnp.float32)[None, :]
    x = rows[...]
    s1 = jnp.sum(x, axis=1, keepdims=True)
    s2 = jnp.sum(x * x, axis=1, keepdims=True)
    lane = lax.broadcasted_iota(jnp.int32, (R, 128), 1)
    st[t] = jnp.where(lane == 0, s1, s2)
    pl.semaphore_wait(barrier, Z + T - 2)

    def stat_copy(k):
        return copy(st.at[t], st.at[t], st_s.at[k - 1], st_r.at[k - 1], "tensor", lax.rem(t + k, T))

    for k in range(1, T):
        stat_copy(k).start()
    for k in range(1, T):
        stat_copy(k).wait_recv()
    total = st[0]
    for k in range(1, T):
        total = total + st[k]
    gain_row = gain[...][None, :]
    mean = total[:, 0:1] / D
    var = total[:, 1:2] / D - mean * mean
    scale = lax.rsqrt(var + 1e-06)
    mine = pl.ds(pl.multiple_of(z * R, R), R)
    for p in range(C):
        cols = slice(p * dlc, (p + 1) * dlc)
        xg[t, p, mine, :] = ((rows[:, cols] - mean) * scale * gain_row[:, cols]).astype(jnp.bfloat16)

    def block(tt, j, p):
        return xg.at[tt, p, pl.ds(pl.multiple_of(lax.rem(z - j + Z, Z) * R, R), R), :]

    def z_copy(s, p):
        b = block(t, s - 1, p)
        return copy(b, b, za_s.at[s - 1, p], za_r.at[s - 1, p], "dp", z_next)

    def y_copy(u, j, p):
        b = block(t_of(u - 1, c), j, p)
        return copy(b, b, ya_s.at[u - 1, j, p], ya_r.at[u - 1, j, p], "tensor", t_next)

    def c_copy(u, j, p):
        b = block(t_of(u, c), j, p)
        return copy(b, b, ca_s.at[u, j, p], ca_r.at[u, j, p], "tensor", t_part)

    def expand(i):
        tt, p = order[i]
        expand_load(i).wait()

        acc = lax.dot_general(
            wv[i], xg[tt, p], (((1,), (1,)), ((), ())), preferred_element_type=jnp.float32
        )
        pre[...] = acc if i == 0 else pre[...] + acc

    def expand_partner(u, p):
        for j in range(Z):
            c_copy(u, j, p).wait_recv()
        expand((2 * u + 1) * C + p)

    def y_arrived(u, j, p):
        y_copy(u, j, p).wait_recv()
        if u < Y - 1:
            y_copy(u + 1, j, p).start()
        c_copy(u, j, p).start()

    for p in range(C):
        z_copy(1, p).start()
        y_copy(1, 0, p).start()
        c_copy(0, 0, p).start()
    for s in range(1, Z):
        for p in range(C):
            z_copy(s, p).wait_recv()
            if s < Z - 1:
                z_copy(s + 1, p).start()
            y_copy(1, s, p).start()
            c_copy(0, s, p).start()
            if s == Z - 1:
                expand(p)
        for p in range(C):
            y_arrived(1, s - 1, p)
    for p in range(C):
        expand_partner(0, p)
    for u in range(1, Y):
        for j in range(Z - 1 if u == 1 else 0, Z):
            for p in range(C):
                y_arrived(u, j, p)
                if j == Z - 1:
                    expand(2 * u * C + p)
                    if p > 0:
                        expand_partner(u, p - 1)
        expand_partner(u, C - 1)

    def activate(n):
        units = slice(None) if nt == hl else pl.ds(pl.multiple_of(n * nt, nt), nt)
        v = pre[units, :].T + bias[:, units]
        hid[:, units] = jax.nn.gelu(v, approximate=True).astype(jnp.bfloat16)

    if nt == hl:
        activate(0)
    else:
        lax.fori_loop(0, hl // nt, lambda n, a: (activate(n), a)[1], 0)

    def cr_copy(u, p):
        return copy(cs.at[u, p], cr.at[u, p], cr_s.at[u, p], cr_r.at[u, p], "tensor", t_part)

    def yr_copy(u, p, h):
        half = slice(h * M // 2, (h + 1) * M // 2)
        return copy(
            ys.at[u - 1, p, half, :], yr.at[u - 1, p, half, :],
            yr_s.at[u - 1, p, h], yr_r.at[u - 1, p, h], "tensor", t_next,
        )

    def zr_copy(k, p):
        there = lax.rem(z + k, Z)
        part = pl.ds(pl.multiple_of(there * R, R), R)
        return copy(zs.at[p, part, :], zr.at[k - 1, p], zr_s.at[k - 1, p], zr_r.at[k - 1, p], "dp", there)

    def columns(p):
        return slice(None) if C2 == 1 else pl.ds(pl.multiple_of(p * w2, w2), w2)

    def product(i, p):
        return jnp.dot(hid[...], rv[i, :, columns(p)], preferred_element_type=jnp.float32)

    def produce(u, p):
        cs[u, p] = product(2 * u + 1, p).astype(jnp.bfloat16)
        cr_copy(u, p).start()
        own[u, p] = product(2 * u, p)

    def combine(u, p):
        cr_copy(u, p).wait_recv()
        v = own[u, p] + cr[u, p].astype(jnp.float32)
        if u == 0:
            ys[0, p] = v.astype(jnp.bfloat16)
            for h in range(2):
                yr_copy(1, p, h).start()
        else:
            own[u, p] = v

    def loop(low, high, body):
        lax.fori_loop(low, high, lambda p, a: (body(p), a)[1], 0)

    for u in range(Y):
        reduce_load(2 * u).wait()
        reduce_load(2 * u + 1).wait()
        produce(u, 0)
        if u > 0:
            combine(u - 1, C2 - 1)

        def step(p):
            produce(u, p)
            combine(u, p - 1)

        if C2 > 1:
            loop(1, C2, step)
    combine(Y - 1, C2 - 1)

    for u in range(1, Y):

        def pass_on(p):
            for h in range(2):
                yr_copy(u, p, h).wait_recv()
                half = slice(h * M // 2, (h + 1) * M // 2)
                v = own[u, p, half, :] + yr[u - 1, p, half, :].astype(jnp.float32)
                if u < Y - 1:
                    ys[u, p, half, :] = v.astype(jnp.bfloat16)
                    yr_copy(u + 1, p, h).start()
                else:
                    own[u, p, half, :] = v
                    zs[p, half, :] = v.astype(jnp.bfloat16)
                    for there in range(h * Z // 2, (h + 1) * Z // 2):

                        @pl.when(there != z)
                        def _():
                            zr_copy(lax.rem(there - z + Z, Z), p).start()

        loop(0, C2, pass_on)

    last[...] = rbias[...][None, :]

    def finish(p):
        acc = own[Y - 1, p, mine, :]
        for k in range(1, Z):
            zr_copy(k, p).wait_recv()
            acc = acc + zr[k - 1, p].astype(jnp.float32)
        cols = columns(p)
        add = acc + last[:, cols]
        top = add.astype(jnp.bfloat16)
        rest = add - top.astype(jnp.float32)
        middle = rest.astype(jnp.bfloat16)
        low = (rest - middle.astype(jnp.float32)).astype(jnp.bfloat16)
        spread = jnp.dot(pick[...], low, preferred_element_type=jnp.float32)
        spread = spread + jnp.dot(pick[...], middle, preferred_element_type=jnp.float32)
        spread = spread + jnp.dot(pick[...], top, preferred_element_type=jnp.float32)
        pt[:, cols] = pt[:, cols] + spread
        save(p).start()

    def save(p):
        cols = columns(p)
        return pltpu.make_async_copy(pt.at[:, cols], out.at[:, cols], osem.at[p])

    loop(0, C2, finish)

    for k in range(1, T):
        stat_copy(k).wait_send()
    for p in range(C):
        for s in range(1, Z):
            z_copy(s, p).wait_send()
        for j in range(Z):
            for u in range(1, Y):
                y_copy(u, j, p).wait_send()
            for u in range(Y):
                c_copy(u, j, p).wait_send()

    def drain(p):
        save(p).wait()
        for u in range(Y):
            cr_copy(u, p).wait_send()
        for u in range(1, Y):
            for h in range(2):
                yr_copy(u, p, h).wait_send()
        for k in range(1, Z):
            zr_copy(k, p).wait_send()

    loop(0, C2, drain)


def body(
    Z, T, patches, counts, ranking, norm_gain, expand_weight, expand_bias, reduce_weight, reduce_bias
):
    images, patch_len, dl = patches.shape
    hl, D = expand_weight.shape
    flat = patches.reshape(images * patch_len, dl)
    R, M, Y = CAP, Z * CAP, T // 2
    C = 3 if dl % 768 == 0 else 1
    w2 = 512 if dl % 512 == 0 else dl
    C2 = dl // w2
    dlc = dl // C
    vmem = pl.BlockSpec(memory_space=pltpu.VMEM)
    hbm = pl.BlockSpec(memory_space=pl.ANY)
    bf16, f32 = jnp.bfloat16, jnp.float32
    dma = pltpu.SemaphoreType.DMA
    N = images * patch_len
    smem = pl.BlockSpec(memory_space=pltpu.SMEM)
    result = pl.pallas_call(
        functools.partial(block_kernel, Z, T, C, C2),
        out_shape=jax.ShapeDtypeStruct((N, dl), f32),
        in_specs=[smem] * 2 + [vmem] * 4 + [hbm] * 3,
        out_specs=hbm,
        scratch_shapes=[
            pltpu.VMEM((N, dl), f32),
            pltpu.VMEM((R, dl), f32),
            pltpu.VMEM((N, R), bf16),
            pltpu.VMEM((T, C, M, dlc), bf16),
            pltpu.VMEM((T * C, hl, dlc), bf16),
            pltpu.VMEM((T, hl, dl), bf16),
            pltpu.VMEM((hl, M), f32),
            pltpu.VMEM((M, hl), bf16),
            pltpu.VMEM((1, hl), f32),
            pltpu.VMEM((1, dl), f32),
            pltpu.VMEM((T, R, 128), f32),
            pltpu.VMEM((Y, C2, M, w2), bf16),
            pltpu.VMEM((Y, C2, M, w2), bf16),
            pltpu.VMEM((Y, C2, M, w2), f32),
            pltpu.VMEM((Y - 1, C2, M, w2), bf16),
            pltpu.VMEM((Y - 1, C2, M, w2), bf16),
            pltpu.VMEM((C2, M, w2), bf16),
            pltpu.VMEM((Z - 1, C2, R, w2), bf16),
            dma, dma((C2,)), dma((T * C,)), dma((T,)),
            dma((T - 1,)), dma((T - 1,)),
            dma((Z - 1, C)), dma((Z - 1, C)),
            dma((Y - 1, Z, C)), dma((Y - 1, Z, C)),
            dma((Y, Z, C)), dma((Y, Z, C)),
            dma((Y, C2)), dma((Y, C2)),
            dma((Y - 1, C2, 2)), dma((Y - 1, C2, 2)),
            dma((Z - 1, C2)), dma((Z - 1, C2)),
        ],
        compiler_params=pltpu.CompilerParams(
            collective_id=0, has_side_effects=True, vmem_limit_bytes=67000000
        ),
        name="feed_forward",
    )(
        counts, ranking, ranking, norm_gain, expand_bias, reduce_bias, flat, expand_weight, reduce_weight,
    )
    return result.reshape(images, patch_len, dl)


def solution(mesh):
    placed = (
        P(("groups", "dp"), None, "tensor"),
        P(("groups", "dp")),
        P(("groups", "dp"), None),
        P("tensor"),
        P(("dp", "tensor"), None),
        P(("dp", "tensor")),
        P(("dp", "tensor"), None),
        P("tensor"),
    )
    return jax.shard_map(
        functools.partial(body, mesh.shape["dp"], mesh.shape["tensor"]),
        mesh=mesh,
        in_specs=placed,
        out_specs=P(("groups", "dp"), None, "tensor"),
        check_vma=False,
    )
```
